256 devices in a mesh: layer: 16 (over z, core), sample: 16 (over y, x).
Axes of the slice: x: 4, y: 4, z: 8, core: 2. Of those that a mesh axis runs over, the one named last changes fastest.
Arguments:
- section_lengths: int32 [16], P('layer'), may hold values from 1 to 4, 40 in all
- forward_states: bfloat16 [16, 16, 32, 32, 128], P('layer', 'sample'), may hold values from -6 to 6
- adjoint_states: bfloat16 [16, 16, 32, 32, 128], P('layer', 'sample'), may hold values from -6 to 6
- weights: bfloat16 [64, 9, 128, 128], P('layer'), may hold values from -0.1875 to 0.1875
- biases: float32 [64, 128], P('layer'), may hold values from -3 to 3
Outputs:
- section_ends: bfloat16 [16, 16, 32, 32, 128], P('layer', 'sample')
- section_starts: bfloat16 [16, 16, 32, 32, 128], P('layer', 'sample')
- weight_grad: float32 [64, 9, 128, 128], P('layer', None, 'sample')
- bias_grad: float32 [64, 128], P('layer', 'sample')
The draws below stay inside these ranges and needn't reach their ends.
Inputs may be any that keep to these rules, and one draw needn't show every extreme that they name: `section_lengths`: the lengths sum to 40, and some section holds exactly 4 layers.
All inputs are finite; a program needn't handle non-finite values. No bound on the sum of `section_lengths` on one device may be relied on, other than what follows from the above.
Results may differ from the reference program's by a relative error of at most 0.02.
Values may be sent and summed in bfloat16 or wider, within the bound.
No kernel may reach another device: no remote copies, remote signals or barrier semaphores. Data moves between devices by JAX's collectives and lax.ppermute only.
A program may use at most 64 MiB of HBM per device.

```python
import math
import jax
import jax.numpy as jnp
import numpy as np
from jax import lax

C = 128
H = 32
W = 32
LMAX = 4
SAMPLES = 16
SLOTS = 64
LAYERS = 40
N_LAYER = 16


def levels(rng, dims, split, smallest, top_value):
    level, own = 1.0, jax.random.fold_in(rng, 6)
    for position, parts in split:
        heights = jnp.exp(jax.random.uniform(jax.random.fold_in(own, position), (parts,), jnp.float32, smallest / len(split), top_value / len(split)))
        level = level * jnp.repeat(heights, dims[position] // parts).reshape([-1 if axis == position else 1 for axis in range(len(dims))])
    return level


def split_up(count, total, limit, slope):
    portions = [(1 << 20) // math.isqrt(rank ** slope) + 1 for rank in range(2, count + 1)]
    spare, counts = total - limit - (count - 1), [1] * (count - 1)
    while spare > 0:
        free = [i for i in range(count - 1) if counts[i] < limit]
        mass, left = sum([portions[i] for i in free]), spare
        for i in free:
            more = min(limit - counts[i], max(1, left * portions[i] // mass), spare)
            counts[i] = counts[i] + more
            spare = spare - more
    return np.array([limit] + counts)


def uneven_parts(rng, count, total, bound, skew):
    if count == 2:
        one = jax.random.randint(rng, (), max(1, total - bound), min(bound, total - 1) + 1)
        return jnp.stack([one, total - one])
    tallies = jnp.asarray(split_up(count, total, bound, skew), jnp.int32)
    couples = (count - 1) // 2
    source_of, taker = tallies[1:1 + 2 * couples:2], tallies[2:2 + 2 * couples:2]
    margin = jnp.minimum(source_of - 1, bound - taker)
    moved = jax.random.randint(jax.random.fold_in(rng, 1), (couples,), 0, 1 << 20) % (margin + 1)
    tallies = tallies.at[1:1 + 2 * couples:2].set(source_of - moved).at[2:2 + 2 * couples:2].set(taker + moved)
    return tallies[jax.random.permutation(jax.random.fold_in(rng, 2), count)]


def scatter_about(rng, extent, deviation, limit, cuts=(), dtype=jnp.bfloat16):
    factor_of = levels(rng, extent, cuts, -0.22, 0.18) if cuts else 1.0
    array = jax.random.normal(rng, extent, jnp.float32) * deviation * factor_of
    return jnp.minimum(jnp.maximum(array, -limit), limit).astype(dtype)


def setup_inputs(seed: int = 0) -> dict:
    splits = jax.random.split(jax.random.key(seed), 6)
    return {
        "section_lengths": uneven_parts(splits[0], N_LAYER, LAYERS, LMAX, 2).astype(jnp.int32),
        "forward_states": scatter_about(splits[1], (N_LAYER, SAMPLES, H, W, C), 1.0, 6.0, ((0, 16), (1, 16))),
        "adjoint_states": scatter_about(splits[2], (N_LAYER, SAMPLES, H, W, C), 1.0, 6.0, ((0, 16), (1, 16))),
        "weights": scatter_about(splits[3], (SLOTS, 9, C, C), (9 * C) ** -0.5, 0.1875, ((0, 16),)),
        "biases": scatter_about(splits[4], (SLOTS, C), 0.5, 3.0, ((0, 16),), jnp.float32),
    }


STEP_SIZE = 0.5

def patches(inputs):
    height, width, channels = (inputs.shape[1], inputs.shape[2], inputs.shape[3])
    padded = jnp.pad(inputs, ((0, 0), (1, 1), (1, 1), (0, 0)))
    windows = [padded[:, row_off:row_off + height, col_off:col_off + width, :] for row_off in range(3) for col_off in range(3)]
    return jnp.concatenate(windows, axis=-1).reshape(-1, 9 * channels)

def run_section(initial, weights, biases, length):
    channels = weights.shape[-1]
    current = initial
    patch_list = []
    tanh_list = []
    for layer_pos in range(weights.shape[0]):
        windows = patches(current.astype(jnp.bfloat16))
        summed = jnp.dot(windows, weights[layer_pos].reshape(9 * channels, channels), preferred_element_type=jnp.float32)
        activity = jnp.tanh(summed + biases[layer_pos])
        advanced = current + STEP_SIZE * activity.reshape(current.shape)
        current = jnp.where(layer_pos < length, advanced, current)
        patch_list.append(windows)
        tanh_list.append(activity)
    return (current, patch_list, tanh_list)

def back_section(terminal, weights, patch_list, tanh_list, length, want_grads):
    channels = weights.shape[-1]
    adjoint = terminal
    count = weights.shape[0]
    weight_terms = [None] * count
    bias_terms = [None] * count
    for layer_pos in reversed(range(count)):
        signal = (STEP_SIZE * adjoint.reshape(-1, channels) * (1.0 - tanh_list[layer_pos] ** 2)).astype(jnp.bfloat16)
        signal = jnp.where(layer_pos < length, signal, jnp.zeros_like(signal))
        flipped = jnp.swapaxes(weights[layer_pos][::-1], 1, 2).reshape(9 * channels, channels)
        back_term = jnp.dot(patches(signal.reshape(adjoint.shape)), flipped, preferred_element_type=jnp.float32)
        adjoint = adjoint + back_term.reshape(adjoint.shape)
        if want_grads:
            weight_terms[layer_pos] = lax.dot_general(patch_list[layer_pos], signal, (((0,), (0,)), ((), ())), preferred_element_type=jnp.float32).reshape(9, channels, channels)
            bias_terms[layer_pos] = lax.optimization_barrier(jnp.sum(signal.astype(jnp.float32), axis=0))
    if want_grads:
        return (adjoint, jnp.stack(weight_terms), jnp.stack(bias_terms))
    return (adjoint, None, None)

def reference(section_lengths, forward_states, adjoint_states, weights, biases):
    sections = section_lengths.shape[0]
    per_section = weights.shape[0] // sections
    channels = weights.shape[-1]
    grouped_w = weights.reshape(sections, per_section, 9, channels, channels)
    grouped_b = biases.reshape(sections, per_section, channels)

    def first_pass(packed):
        initial, sec_w, sec_b, length = packed
        return run_section(initial.astype(jnp.float32), sec_w, sec_b, length)[0].astype(jnp.bfloat16)
    propagated = lax.map(first_pass, (forward_states, grouped_w, grouped_b, section_lengths))
    relaxed_states = jnp.concatenate([forward_states[:1], propagated[:-1]], axis=0)

    def second_pass(packed):
        initial, terminal, sec_w, sec_b, length = packed
        ending, patch_list, tanh_list = run_section(initial.astype(jnp.float32), sec_w, sec_b, length)
        adjoint = back_section(terminal.astype(jnp.float32), sec_w, patch_list, tanh_list, length, False)[0]
        return (ending.astype(jnp.bfloat16), adjoint.astype(jnp.bfloat16))
    section_ends, back_starts = lax.map(second_pass, (relaxed_states, adjoint_states, grouped_w, grouped_b, section_lengths))
    relaxed_adjoints = jnp.concatenate([back_starts[1:], adjoint_states[-1:]], axis=0)

    def third_pass(packed):
        initial, terminal, sec_w, sec_b, length = packed
        ending, patch_list, tanh_list = run_section(initial.astype(jnp.float32), sec_w, sec_b, length)
        adjoint, weight_terms, bias_terms = back_section(terminal.astype(jnp.float32), sec_w, patch_list, tanh_list, length, True)
        return (adjoint.astype(jnp.bfloat16), weight_terms, bias_terms)
    section_starts, weight_terms, bias_terms = lax.map(third_pass, (relaxed_states, relaxed_adjoints, grouped_w, grouped_b, section_lengths))
    factor = 1.0 / math.sqrt(forward_states.shape[1] * forward_states.shape[2] * forward_states.shape[3])
    weight_grad = (weight_terms * factor).reshape(weights.shape)
    bias_grad = (bias_terms * factor).reshape(biases.shape)
    return (section_ends, section_starts, weight_grad, bias_grad)
```

```python
import functools
import math

import jax
import jax.numpy as jnp
from jax import lax
from jax.experimental import pallas as pl
from jax.experimental.pallas import tpu as pltpu
from jax.sharding import PartitionSpec as P

STEP_SIZE = 0.5
C = 128
LMAX = 4
TAPS = 9
F32 = jnp.float32
BF16 = jnp.bfloat16
LEFT = 8


def shift_by(block, axis, distance):
    devices = range(lax.axis_size(axis))
    route = [(i - distance, i) for i in devices if i - distance in devices]
    return lax.ppermute(block, axis, route)


def clear_edges(wide, fan):
    edge = jnp.zeros((16, 2, 8, C), F32)
    wide[:, :, 0:8, :] = edge
    wide[:, :, 40:48, :] = edge
    line = jnp.zeros((32, 3 * C), BF16)
    fan[0, 0] = line
    fan[16, 1] = line


def spread(wide, fan):
    for dx in range(3):
        lanes = slice(dx * C, (dx + 1) * C)
        columns = slice(LEFT - 1 + dx, LEFT + 31 + dx)
        fan[0:16, 1, :, lanes] = wide[:, 0, columns, :].astype(BF16)
        fan[1:17, 0, :, lanes] = wide[:, 1, columns, :].astype(BF16)


def row_window(fan, row, lanes=slice(0, 3 * C)):
    return fan[row // 2 : row // 2 + 16, row % 2, :, lanes].reshape(512, -1)


def convolve(fan, matrix, transposed):
    rows = jnp.concatenate([row_window(fan, row) for row in range(4)], axis=1)
    dims = (((1,), (1 if transposed else 0,)), ((), ()))
    return lax.dot_general(rows, matrix, dims, preferred_element_type=F32)


def forward_matrix(w):
    zero = jnp.zeros((C, C), BF16)
    columns = []
    for out in range(2):
        blocks = [
            w[3 * (row - out) + dx] if 0 <= row - out <= 2 else zero
            for row in range(4)
            for dx in range(3)
        ]
        columns.append(jnp.concatenate(blocks, axis=0))
    return jnp.concatenate(columns, axis=1)


def backward_matrix(w):
    zero = jnp.zeros((C, C), BF16)
    rows = []
    for out in range(2):
        blocks = [
            w[8 - 3 * (row - out) - dx] if 0 <= row - out <= 2 else zero
            for row in range(4)
            for dx in range(3)
        ]
        rows.append(jnp.concatenate(blocks, axis=1))
    return jnp.concatenate(rows, axis=0)


def forward_layer(w, bias, wide, fan, slope=None):
    z = convolve(fan, forward_matrix(w), False) + jnp.concatenate([bias, bias], axis=1)
    t = jnp.tanh(z)
    for half in range(2):
        part = t[:, half * C : (half + 1) * C].reshape(16, 32, C)
        wide[:, half, LEFT : LEFT + 32, :] += STEP_SIZE * part
        if slope is not None:
            slope[:, half] = STEP_SIZE * (1.0 - part * part)


def backward_layer(w, wide, fan, adjoint, slope):
    wide[:, :, LEFT : LEFT + 32, :] = adjoint[...] * slope[...]
    spread(wide, fan)
    back = convolve(fan, backward_matrix(w), True)
    for half in range(2):
        adjoint[:, half] += back[:, half * C : (half + 1) * C].reshape(16, 32, C)


def first_kernel(length, state, w, bias, out, wide, fan):
    j = pl.program_id(0)

    @pl.when(j == 0)
    def _():
        clear_edges(wide, fan)
        wide[:, :, LEFT : LEFT + 32, :] = state[...].astype(F32)

    @pl.when(j < length[0])
    def _():
        spread(wide, fan)
        forward_layer(w.at[0], bias[pl.ds(j, 1), :], wide, fan)

    @pl.when(j == LMAX - 1)
    def _():
        out[...] = wide[:, :, LEFT : LEFT + 32, :].astype(BF16)


def second_kernel(
    length, given, received, terminal, w, bias, ending, back, states, slopes, wide, fan, kept, adjoint
):
    step = pl.program_id(0)
    leading = lax.axis_index("layer") == 0

    @pl.when(step == 0)
    def _():
        clear_edges(wide, fan)
        adjoint[...] = terminal[...].astype(F32)

    @pl.when(jnp.logical_and(step == 0, leading))
    def _():
        wide[:, :, LEFT : LEFT + 32, :] = given[...].astype(F32)

    @pl.when(jnp.logical_and(step == 0, jnp.logical_not(leading)))
    def _():
        wide[:, :, LEFT : LEFT + 32, :] = received[...].astype(F32)

    @pl.when(step < length[0])
    def _():
        spread(wide, fan)
        states[0, :, 0] = fan[0:16, 1, :, C : 2 * C]
        states[0, :, 1] = fan[1:17, 0, :, C : 2 * C]
        forward_layer(w.at[0], bias[pl.ds(step, 1), :], wide, fan, kept.at[step])
        slopes[0] = kept[step]

    @pl.when(step == LMAX - 1)
    def _():
        ending[...] = wide[:, :, LEFT : LEFT + 32, :].astype(BF16)

    slot = 2 * LMAX - 1 - step

    @pl.when(jnp.logical_and(step >= LMAX, slot < length[0]))
    def _():
        backward_layer(w.at[0], wide, fan, adjoint, kept.at[slot])

    @pl.when(step == 2 * LMAX - 1)
    def _():
        back[...] = adjoint[...].astype(BF16)


def turn_kernel(length, states, turned, wide):
    j = pl.program_id(0)

    @pl.when(j == 0)
    def _():
        edge = jnp.zeros((16, 2, 8, C), F32)
        wide[:, :, 0:8, :] = edge
        wide[:, :, 40:48, :] = edge

    @pl.when(j < length[0])
    def _():
        wide[:, :, LEFT : LEFT + 32, :] = states[0].astype(F32)
        for dx in range(3):
            for half in range(2):
                part = wide[:, half, LEFT - 1 + dx : LEFT + 31 + dx, :].reshape(512, C)
                turned[0, dx * C : (dx + 1) * C, half * 512 : (half + 1) * 512] = part.astype(BF16).T


def third_kernel(
    length, given, received, w, turned, slopes, start, grads, wide, fan, adjoint, sums
):
    step = pl.program_id(0)
    slot = LMAX - 1 - step
    trailing = lax.axis_index("layer") == lax.axis_size("layer") - 1

    @pl.when(step == 0)
    def _():
        clear_edges(wide, fan)
        sums[...] = jnp.zeros_like(sums)

    @pl.when(jnp.logical_and(step == 0, trailing))
    def _():
        adjoint[...] = given[...].astype(F32)

    @pl.when(jnp.logical_and(step == 0, jnp.logical_not(trailing)))
    def _():
        adjoint[...] = received[...].astype(F32)

    @pl.when(slot < length[0])
    def _():
        backward_layer(w.at[0], wide, fan, adjoint, slopes.at[0])
        middle = slice(C, 2 * C)
        signals = jnp.concatenate(
            [
                jnp.concatenate([row_window(fan, half + 2 - dy, middle) for dy in range(3)], axis=1)
                for half in range(2)
            ],
            axis=0,
        )
        total = jnp.dot(turned[0], signals, preferred_element_type=F32)
        for dy in range(3):
            for dx in range(3):
                block = total[dx * C : (dx + 1) * C, dy * C : (dy + 1) * C]
                grads[:, slot * TAPS + 3 * dy + dx] = block.reshape(16, 8, C).astype(BF16)
        sums[pl.ds(slot, 1), :] = jnp.sum(
            signals[:, C : 2 * C].astype(F32), axis=0, keepdims=True
        )

    @pl.when(slot >= length[0])
    def _():
        grads[:, pl.ds(slot * TAPS, TAPS)] = jnp.zeros((16, TAPS, 8, C), BF16)

    @pl.when(step == LMAX - 1)
    def _():
        start[...] = adjoint[...].astype(BF16)
        grads[:, LMAX * TAPS] = jnp.broadcast_to(sums[...][None], (16, 8, C)).astype(BF16)


IMAGE = (16, 2, 32, C)
WIDE = pltpu.VMEM((16, 2, 48, C), F32)
FAN = pltpu.VMEM((17, 2, 32, 3 * C), BF16)
CONV_FLOPS = 2 * 1024 * 9 * C * C


def whole(shape):
    return pl.BlockSpec(shape, lambda *_: (0,) * len(shape))


def slotted(shape, slot_of):
    rest = (0,) * len(shape)
    return pl.BlockSpec((1,) + shape, lambda step, *_: (slot_of(step),) + rest)


def call(kernel, name, steps, ins, outs, shapes, scratch, flops):
    return pl.pallas_call(
        kernel,
        name=name,
        out_shape=shapes,
        grid_spec=pltpu.PrefetchScalarGridSpec(
            num_scalar_prefetch=1, grid=(steps,), in_specs=ins, out_specs=outs, scratch_shapes=scratch
        ),
        compiler_params=pltpu.CompilerParams(
            dimension_semantics=("arbitrary",), vmem_limit_bytes=40 * 2**20
        ),
        cost_estimate=pl.CostEstimate(flops=flops, bytes_accessed=4 * 2**20, transcendentals=0),
    )


def body(section_lengths, forward_states, adjoint_states, weights, biases):
    given_state = forward_states.reshape(IMAGE)
    given_adjoint = adjoint_states.reshape(IMAGE)
    image = jax.ShapeDtypeStruct(IMAGE, BF16)
    taps = (TAPS, C, C)
    up = slotted(taps, lambda step: step)
    down = slotted(taps, lambda step: LMAX - 1 - step)

    propagated = call(
        first_kernel, "first", LMAX,
        [whole(IMAGE), up, whole((LMAX, C))],
        whole(IMAGE), image, [WIDE, FAN], LMAX * CONV_FLOPS,
    )(section_lengths, given_state, weights, biases)
    received = shift_by(propagated, "layer", 1)

    ending, back_start, states, slopes = call(
        second_kernel, "second", 2 * LMAX,
        [
            whole(IMAGE), whole(IMAGE), whole(IMAGE),
            slotted(taps, lambda step: jnp.minimum(step, 2 * LMAX - 1 - step)),
            whole((LMAX, C)),
        ],
        [
            whole(IMAGE), whole(IMAGE),
            slotted(IMAGE, lambda step: jnp.minimum(step, LMAX - 1)),
            slotted(IMAGE, lambda step: jnp.minimum(step, LMAX - 1)),
        ],
        [
            image, image,
            jax.ShapeDtypeStruct((LMAX,) + IMAGE, BF16),
            jax.ShapeDtypeStruct((LMAX,) + IMAGE, F32),
        ],
        [WIDE, FAN, pltpu.VMEM((LMAX,) + IMAGE, F32), pltpu.VMEM(IMAGE, F32)],
        2 * LMAX * CONV_FLOPS,
    )(section_lengths, given_state, received, given_adjoint, weights, biases)
    received_back = shift_by(back_start, "layer", -1)

    turned = call(
        turn_kernel, "turn", LMAX,
        [slotted(IMAGE, lambda step: step)],
        slotted((3 * C, 1024), lambda step: step),
        jax.ShapeDtypeStruct((LMAX, 3 * C, 1024), BF16),
        [WIDE], 10**6,
    )(section_lengths, states)

    starting, grads = call(
        third_kernel, "third", LMAX,
        [
            whole(IMAGE), whole(IMAGE), down,
            slotted((3 * C, 1024), lambda step: LMAX - 1 - step),
            slotted(IMAGE, lambda step: LMAX - 1 - step),
        ],
        [whole(IMAGE), whole((16, LMAX * TAPS + 1, 8, C))],
        [image, jax.ShapeDtypeStruct((16, LMAX * TAPS + 1, 8, C), BF16)],
        [WIDE, FAN, pltpu.VMEM(IMAGE, F32), pltpu.VMEM((8, C), F32)],
        2 * LMAX * CONV_FLOPS,
    )(section_lengths, given_adjoint, received_back, weights, turned, slopes)

    pieces = lax.all_to_all(grads, "sample", 0, 0)
    total_samples = forward_states.shape[1] * lax.axis_size("sample")
    factor = 1.0 / math.sqrt(total_samples * forward_states.shape[2] * forward_states.shape[3])
    total = jnp.sum(pieces.astype(F32), axis=0) * factor
    weight_part = total[: LMAX * TAPS].reshape(LMAX, TAPS, 8, C)
    bias_part = lax.dynamic_slice_in_dim(total[LMAX * TAPS, :LMAX], 8 * lax.axis_index("sample"), 8, 1)
    shape = forward_states.shape
    return (ending.reshape(shape), starting.reshape(shape), weight_part, bias_part)


def solution(mesh):
    placed = (
        P("layer"),
        P("layer", "sample", None, None, None),
        P("layer", "sample", None, None, None),
        P("layer", None, None, None),
        P("layer", None),
    )
    return jax.shard_map(
        body,
        mesh=mesh,
        in_specs=placed,
        out_specs=(
            P("layer", "sample", None, None, None),
            P("layer", "sample", None, None, None),
            P("layer", None, "sample", None),
            P("layer", "sample"),
        ),
        check_vma=False,
    )
```

```python
import functools
import math

import jax
import jax.numpy as jnp
from jax import lax
from jax.experimental import pallas as pl
from jax.experimental.pallas import tpu as pltpu
from jax.sharding import PartitionSpec as P


STEP_SIZE = 0.5
C = 128
LMAX = 4
HALF = 2
SIDE = 4
TAPS = 9
F32 = jnp.float32
BF16 = jnp.bfloat16
LEFT = 8


def shift_by(block, axis, distance):
    count = lax.axis_size(axis)
    return lax.ppermute(block, axis, [(i, (i + distance) % count) for i in range(count)])


def send_ahead(block, along_x, distance):
    route = []
    for y in range(SIDE):
        for x in range(SIDE):
            to = (y, (x + distance) % SIDE) if along_x else ((y + distance) % SIDE, x)
            route.append((SIDE * y + x, SIDE * to[0] + to[1]))
    return lax.ppermute(block, "sample", route)


def clear_edges(wide, fan):
    edge = jnp.zeros((16, 2, 8, C), F32)
    wide[:, :, 0:8, :] = edge
    wide[:, :, 40:48, :] = edge
    line = jnp.zeros((32, 3 * C), BF16)
    fan[0, 0] = line
    fan[16, 1] = line


def spread(wide, fan):
    for dx in range(3):
        lanes = slice(dx * C, (dx + 1) * C)
        columns = slice(LEFT - 1 + dx, LEFT + 31 + dx)
        fan[0:16, 1, :, lanes] = wide[:, 0, columns, :].astype(BF16)
        fan[1:17, 0, :, lanes] = wide[:, 1, columns, :].astype(BF16)


def row_window(fan, row, lanes=slice(0, 3 * C)):
    return fan[row // 2 : row // 2 + 16, row % 2, :, lanes].reshape(512, -1)


def convolve(fan, w):
    rows = jnp.concatenate([row_window(fan, row) for row in range(4)], axis=1)
    return jnp.dot(rows, paired_matrix(w), preferred_element_type=F32)


def paired_matrix(w):
    zero = jnp.zeros((C, C), BF16)
    columns = []
    for out in range(2):
        blocks = [
            w[3 * (row - out) + dx] if 0 <= row - out <= 2 else zero
            for row in range(4)
            for dx in range(3)
        ]
        columns.append(jnp.concatenate(blocks, axis=0))
    return jnp.concatenate(columns, axis=1)


def forward_layer(w, bias, wide, fan, slope=None):
    z = convolve(fan, w) + jnp.concatenate([bias, bias], axis=1)
    t = jnp.tanh(z)
    for half in range(2):
        part = t[:, half * C : (half + 1) * C].reshape(16, 32, C)
        wide[:, half, LEFT : LEFT + 32, :] += STEP_SIZE * part
        if slope is not None:
            slope[:, half] = STEP_SIZE * (1.0 - part * part)


def backward_layer(w, wide, fan, adjoint, slope):
    wide[:, :, LEFT : LEFT + 32, :] = adjoint[...] * slope[...]
    spread(wide, fan)
    back = convolve(fan, w)
    for half in range(2):
        adjoint[:, half] += back[:, half * C : (half + 1) * C].reshape(16, 32, C)


def first_kernel(length, state, w, bias, out, wide, fan, state_in, w_in, bias_in, sems):
    j = pl.program_id(0)
    load_state = pltpu.make_async_copy(state, state_in, sems.at[LMAX])
    load_bias = pltpu.make_async_copy(bias, bias_in, sems.at[LMAX + 1])

    def load_weights(slot):
        return pltpu.make_async_copy(w.at[slot], w_in.at[slot], sems.at[slot])

    @pl.when(j == 0)
    def _():
        load_state.start()
        load_weights(0).start()
        load_bias.start()
        clear_edges(wide, fan)
        load_state.wait()
        wide[:, :, LEFT : LEFT + 32, :] = state_in[...].astype(F32)
        load_bias.wait()

    for slot in range(LMAX):

        @pl.when(j == slot)
        def _():
            load_weights(slot).wait()
            if slot == 0:
                for later in range(1, LMAX):
                    load_weights(later).start()

    @pl.when(j < length[0])
    def _():
        spread(wide, fan)
        forward_layer(w_in.at[j], bias_in[pl.ds(j, 1), :], wide, fan)

    @pl.when(j == LMAX - 1)
    def _():
        out[...] = wide[:, :, LEFT : LEFT + 32, :].astype(BF16)


def prepare_kernel(length, w, ahead, behind):
    ahead[...] = w[...]
    for tap in range(TAPS):
        behind[0, tap] = w[0, TAPS - 1 - tap].T


def second_kernel(
    length, given, received, terminal, ahead, behind, bias, ending, back, states, slopes, wide, fan, kept, adjoint
):
    step = pl.program_id(0)
    leading = lax.axis_index("layer") == 0

    @pl.when(step == 0)
    def _():
        clear_edges(wide, fan)
        adjoint[...] = terminal[...].astype(F32)

    @pl.when(jnp.logical_and(step == 0, leading))
    def _():
        wide[:, :, LEFT : LEFT + 32, :] = given[...].astype(F32)

    @pl.when(jnp.logical_and(step == 0, jnp.logical_not(leading)))
    def _():
        wide[:, :, LEFT : LEFT + 32, :] = received[...].astype(F32)

    @pl.when(step < length[0])
    def _():
        spread(wide, fan)
        states[0, :, 0] = fan[0:16, 1, :, C : 2 * C]
        states[0, :, 1] = fan[1:17, 0, :, C : 2 * C]
        forward_layer(ahead.at[0], bias[pl.ds(step, 1), :], wide, fan, kept.at[step])
        slopes[0] = kept[step]

    @pl.when(step == LMAX - 1)
    def _():
        ending[...] = wide[:, :, LEFT : LEFT + 32, :].astype(BF16)

    slot = 2 * LMAX - 1 - step

    @pl.when(jnp.logical_and(step >= LMAX, slot < length[0]))
    def _():
        backward_layer(behind.at[0], wide, fan, adjoint, kept.at[slot])

    @pl.when(step == 2 * LMAX - 1)
    def _():
        back[...] = adjoint[...].astype(BF16)


def turn_kernel(length, states, turned, wide):
    j = pl.program_id(0)

    @pl.when(j == 0)
    def _():
        edge = jnp.zeros((16, 2, 8, C), F32)
        wide[:, :, 0:8, :] = edge
        wide[:, :, 40:48, :] = edge

    @pl.when(j < length[0])
    def _():
        wide[:, :, LEFT : LEFT + 32, :] = states[0].astype(F32)
        for dx in range(3):
            for half in range(2):
                part = wide[:, half, LEFT - 1 + dx : LEFT + 31 + dx, :].reshape(512, C)
                turned[0, dx * C : (dx + 1) * C, half * 512 : (half + 1) * 512] = part.astype(BF16).T


def gradient_layer(slot, length, w, turned, slope, wide, fan, adjoint, sums, total):
    @pl.when(slot < length[0])
    def _():
        backward_layer(w, wide, fan, adjoint, slope)
        middle = slice(C, 2 * C)
        signals = jnp.concatenate(
            [
                jnp.concatenate([row_window(fan, half + 2 - dy, middle) for dy in range(3)], axis=1)
                for half in range(2)
            ],
            axis=0,
        )
        total[...] = jnp.dot(turned, signals, preferred_element_type=F32)
        sums[pl.ds(slot, 1), :] = jnp.sum(
            signals[:, C : 2 * C].astype(F32), axis=0, keepdims=True
        )

    @pl.when(slot >= length[0])
    def _():
        total[...] = jnp.zeros_like(total)


def third_kernel(length, given, received, w, turned, slopes, adjoint, sums, *rest):
    messages, (wide, fan, total) = rest[:SIDE], rest[SIDE:]
    sample = lax.axis_index("sample")
    x, y = lax.rem(sample, SIDE), sample // SIDE
    step = pl.program_id(0)
    slot = LMAX - 1 - step
    trailing = lax.axis_index("layer") == lax.axis_size("layer") - 1

    @pl.when(step == 0)
    def _():
        clear_edges(wide, fan)
        sums[...] = jnp.zeros_like(sums)

    @pl.when(jnp.logical_and(step == 0, trailing))
    def _():
        adjoint[...] = given[...].astype(F32)

    @pl.when(jnp.logical_and(step == 0, jnp.logical_not(trailing)))
    def _():
        adjoint[...] = received[...].astype(F32)

    gradient_layer(
        slot, length, w.at[0], turned[0], slopes.at[0], wide, fan, adjoint, sums, total
    )
    base = (slot - HALF) * TAPS
    for right in range(SIDE):
        for down in range(SIDE):
            target = SIDE * lax.rem(y + down, SIDE) + lax.rem(x + right, SIDE)
            for dy in range(3):
                for dx in range(3):
                    rows = pl.ds(pl.multiple_of(dx * C + 8 * target, 8), 8)
                    block = total[rows, dy * C : (dy + 1) * C]
                    messages[right][down, base + 3 * dy + dx] = block.astype(BF16)


def merge_kernel(own, right, across, left, *outs):
    total = own[...].astype(F32) + right[...].astype(F32)
    total = total + across[...].astype(F32) + left[...].astype(F32)
    outs[0][...] = total[0]
    for down in range(1, SIDE):
        outs[down][...] = total[down].astype(BF16)


def fourth_kernel(
    length, adjoint_in, sums_in, w, turned, slopes, start, grads, wide, fan, adjoint, sums, total
):
    step = pl.program_id(0)
    slot = HALF - 1 - step

    @pl.when(step == 0)
    def _():
        clear_edges(wide, fan)
        sums[...] = sums_in[...]
        adjoint[...] = adjoint_in[...]

    gradient_layer(
        slot, length, w.at[0], turned[0], slopes.at[0], wide, fan, adjoint, sums, total
    )
    for dy in range(3):
        for dx in range(3):
            block = total[dx * C : (dx + 1) * C, dy * C : (dy + 1) * C]
            grads[:, slot * TAPS + 3 * dy + dx] = block.reshape(16, 8, C).astype(BF16)

    @pl.when(step == HALF - 1)
    def _():
        start[...] = adjoint[...].astype(BF16)
        for target in range(16):
            grads[target, HALF * TAPS] = pltpu.roll(sums[...], (C - 8 * target) % C, 1).astype(BF16)


def finish_kernel(factor, late, own, one, two, three, weight, bias):
    total = jnp.sum(late[...].astype(F32), axis=0) * factor
    weight[: HALF * TAPS] = total[: HALF * TAPS]
    bias[...] = total[HALF * TAPS, :LMAX, :8]
    early = own[...] + one[...].astype(F32) + two[...].astype(F32) + three[...].astype(F32)
    weight[HALF * TAPS :] = early * factor


IMAGE = (16, 2, 32, C)
WIDE = pltpu.VMEM((16, 2, 48, C), F32)
FAN = pltpu.VMEM((17, 2, 32, 3 * C), BF16)
CONV_FLOPS = 2 * 1024 * 9 * C * C


def whole(shape):
    return pl.BlockSpec(shape, lambda *_: (0,) * len(shape))


def slotted(shape, slot_of):
    rest = (0,) * len(shape)
    return pl.BlockSpec((1,) + shape, lambda step, *_: (slot_of(step),) + rest)


def call(kernel, steps, ins, outs, shapes, scratch, flops, vmem=14 * 2**20):
    return pl.pallas_call(
        kernel,
        out_shape=shapes,
        grid_spec=pltpu.PrefetchScalarGridSpec(
            num_scalar_prefetch=1, grid=(steps,), in_specs=ins, out_specs=outs, scratch_shapes=scratch
        ),
        compiler_params=pltpu.CompilerParams(
            dimension_semantics=("arbitrary",), vmem_limit_bytes=vmem
        ),
        cost_estimate=pl.CostEstimate(flops=flops, bytes_accessed=4 * 2**20, transcendentals=0),
    )


def body(section_lengths, forward_states, adjoint_states, weights, biases):
    given_state = forward_states.reshape(IMAGE)
    given_adjoint = adjoint_states.reshape(IMAGE)
    image = jax.ShapeDtypeStruct(IMAGE, BF16)
    taps = (TAPS, C, C)
    up = slotted(taps, lambda step: step)
    down = slotted(taps, lambda step: LMAX - 1 - step)

    hbm = pl.BlockSpec(memory_space=pltpu.HBM)
    propagated = call(
        first_kernel, LMAX,
        [hbm, hbm, hbm],
        whole(IMAGE), image,
        [
            WIDE, FAN, pltpu.VMEM(IMAGE, BF16), pltpu.VMEM((LMAX,) + taps, BF16),
            pltpu.VMEM((LMAX, C), F32), pltpu.SemaphoreType.DMA((LMAX + 2,)),
        ],
        LMAX * CONV_FLOPS, 63 * 2**20,
    )(section_lengths, given_state, weights, biases)
    received = shift_by(propagated, "layer", 1)

    weights_like = jax.ShapeDtypeStruct((LMAX,) + taps, BF16)
    ahead, behind = call(
        prepare_kernel, LMAX, [up], [up, up], [weights_like, weights_like], [], 10**6
    )(section_lengths, weights)

    ending, back_start, states, slopes = call(
        second_kernel, 2 * LMAX,
        [
            whole(IMAGE), whole(IMAGE), whole(IMAGE),
            slotted(taps, lambda step: jnp.minimum(step, LMAX - 1)),
            slotted(taps, lambda step: jnp.minimum(2 * LMAX - 1 - step, LMAX - 1)),
            whole((LMAX, C)),
        ],
        [
            whole(IMAGE), whole(IMAGE),
            slotted(IMAGE, lambda step: jnp.minimum(step, LMAX - 1)),
            slotted(IMAGE, lambda step: jnp.minimum(step, LMAX - 1)),
        ],
        [
            image, image,
            jax.ShapeDtypeStruct((LMAX,) + IMAGE, BF16),
            jax.ShapeDtypeStruct((LMAX,) + IMAGE, F32),
        ],
        [WIDE, FAN, pltpu.VMEM((LMAX,) + IMAGE, F32), pltpu.VMEM(IMAGE, F32)],
        2 * LMAX * CONV_FLOPS,
    )(section_lengths, given_state, received, given_adjoint, ahead, behind, biases)
    received_back = shift_by(back_start, "layer", -1)

    turned = call(
        turn_kernel, LMAX,
        [slotted(IMAGE, lambda step: step)],
        slotted((3 * C, 1024), lambda step: step),
        jax.ShapeDtypeStruct((LMAX, 3 * C, 1024), BF16),
        [WIDE], 10**6,
    )(section_lengths, states)

    middle = jax.ShapeDtypeStruct(IMAGE, F32)
    tally = jax.ShapeDtypeStruct((8, C), F32)
    message = (SIDE, HALF * TAPS, 8, C)
    total = pltpu.VMEM((3 * C, 3 * C), F32)
    adjoint, sums, *messages = call(
        third_kernel, HALF,
        [
            whole(IMAGE), whole(IMAGE), down,
            slotted((3 * C, 1024), lambda step: LMAX - 1 - step),
            slotted(IMAGE, lambda step: LMAX - 1 - step),
        ],
        [whole(IMAGE), whole((8, C))] + [whole(message)] * SIDE,
        [middle, tally] + [jax.ShapeDtypeStruct(message, BF16)] * SIDE,
        [WIDE, FAN, total],
        2 * HALF * CONV_FLOPS,
    )(section_lengths, given_adjoint, received_back, behind, turned, slopes)
    got = []
    for k in (1, 2, 3):
        got.append(send_ahead(messages[k], True, k))

    starting, grads = call(
        fourth_kernel, HALF,
        [
            whole(IMAGE), whole((8, C)),
            slotted(taps, lambda step: HALF - 1 - step),
            slotted((3 * C, 1024), lambda step: HALF - 1 - step),
            slotted(IMAGE, lambda step: HALF - 1 - step),
        ],
        [whole(IMAGE), whole((16, HALF * TAPS + 1, 8, C))],
        [image, jax.ShapeDtypeStruct((16, HALF * TAPS + 1, 8, C), BF16)],
        [WIDE, FAN, pltpu.VMEM(IMAGE, F32), pltpu.VMEM((8, C), F32), total],
        2 * HALF * CONV_FLOPS,
    )(section_lengths, adjoint, sums, behind, turned, slopes)
    late = lax.all_to_all(grads, "sample", 0, 0)

    piece = message[1:]
    merged = pl.pallas_call(
        merge_kernel,
        name="merge",
        out_shape=[jax.ShapeDtypeStruct(piece, F32)] + [jax.ShapeDtypeStruct(piece, BF16)] * 3,
        compiler_params=pltpu.CompilerParams(vmem_limit_bytes=16 * 2**20),
    )(messages[0], *got)
    early = [merged[0]] + [send_ahead(merged[k], False, k) for k in (1, 2, 3)]

    total_samples = forward_states.shape[1] * lax.axis_size("sample")
    factor = 1.0 / math.sqrt(total_samples * forward_states.shape[2] * forward_states.shape[3])
    weight_part, bias_part = pl.pallas_call(
        functools.partial(finish_kernel, factor),
        name="finish",
        out_shape=(
            jax.ShapeDtypeStruct((LMAX * TAPS, 8, C), F32),
            jax.ShapeDtypeStruct((LMAX, 8), F32),
        ),
        compiler_params=pltpu.CompilerParams(vmem_limit_bytes=16 * 2**20),
    )(late, *early)
    weight_part = weight_part.reshape(LMAX, TAPS, 8, C)
    shape = forward_states.shape
    return (ending.reshape(shape), starting.reshape(shape), weight_part, bias_part)


def solution(mesh):
    placed = (
        P("layer"),
        P("layer", "sample", None, None, None),
        P("layer", "sample", None, None, None),
        P("layer", None, None, None),
        P("layer", None),
    )
    return jax.shard_map(
        body,
        mesh=mesh,
        in_specs=placed,
        out_specs=(
            P("layer", "sample", None, None, None),
            P("layer", "sample", None, None, None),
            P("layer", None, "sample", None),
            P("layer", "sample"),
        ),
        check_vma=False,
    )
```
